32 devices in a mesh: group: 2 (over y), seq: 4 (over z), mp: 4 (over x, core).
Axes of the slice: x: 2, y: 2, z: 4, core: 2. Of those that a mesh axis runs over, the one named last changes fastest.
Arguments:
- embeds: bfloat16 [8192, 8192], P('seq', 'mp'), may hold values from -250 to 250
- image_feats: bfloat16 [512, 7296], P('seq'), may hold values from -6 to 6
- image_pos: int32 [512], P('seq'), may hold values from 0 to 8191, as said below
- proj_w: bfloat16 [7296, 8192], P('seq', 'mp'), may hold values from -0.0625 to 0.0625
- proj_b: bfloat16 [8192], P('mp'), may hold values from -3 to 3
- norm_gain: bfloat16 [8192], P('mp'), may hold values from 0.099609375 to 1.8984375
- kv_w: bfloat16 [8192, 2048], P('mp'), may hold values from -0.0625 to 0.0625
- prompt_lengths: int32 [2], replicated, may hold values from 2048 to 4096
- page_owner: int32 [512, 1], P('seq'), may hold values from 0 to 3; in each aligned block of 128 rows (0 to 127, 128 to 255, ...) at most 64 rows name the same one
- queries: bfloat16 [512, 8192], P('seq', 'mp'), may hold values from -180 to 180
- kv_cache: bfloat16 [512, 128, 2048], P('seq', None, 'mp'), may hold values from -5 to 5
- new_kv: bfloat16 [512, 2048], P('seq', 'mp'), may hold values from -5 to 5
- cache_lengths: int32 [512], P('seq'), may hold values from 2 to 128
Outputs:
- page_slots: bfloat16 [2048, 16, 2048], P(('group', 'seq'), None, 'mp')
- row_states: bfloat16 [1024, 8192], P(('group', 'seq'), 'mp')
The draws below stay inside these ranges and needn't reach their ends.
Inputs may be any that keep to these rules, and one draw needn't show every extreme that they name: `image_pos`: distinct and increasing; entries s * 128 to (s + 1) * 128 - 1 lie among tokens s * 2048 to (s + 1) * 2048 - 1. `page_owner`: among the 128 pages of one seq index no owner is named more than 64 times.
All inputs are finite; a program needn't handle non-finite values.
Results may differ from the reference program's by a relative error of at most 0.005.
Values may be sent and summed in bfloat16 or wider, within the bound.
A program may use at most 128 MiB of HBM per device.

```python
import math
import jax
import jax.numpy as jnp
import numpy as np
from jax import lax

D = 8192
QH = 64
KVH = 8
HEAD = 128
C_VIS = 7296
PAGE = 16
PROMPT_LEN = 4096
ROWS_DEV = 2048
BATCH_DEV = 128
CACHE = 128
TOKENS = 8192
IMGS = 512
PROMPTS = 2
PAGES_DEV = 128
PAGES = 512
CAP = 64
N_SEQ = 4


def decode_pair(key):
    cache_key = jax.random.fold_in(key, 11)
    query_key = jax.random.fold_in(key, 12)
    stored = jnp.clip(jax.random.normal(cache_key, (IMGS, CACHE, KVH, 2, HEAD), jnp.float32), -5.0, 5.0)
    asked = jnp.clip(jax.random.normal(query_key, (IMGS, KVH, QH // KVH, HEAD), jnp.float32), -5.0, 5.0)
    return (stored.reshape(IMGS, CACHE, KVH * 2 * HEAD), asked.reshape(IMGS, QH * HEAD))


def draw_kv_cache(key, part):
    return decode_pair(key)[0].astype(jnp.bfloat16)


def draw_queries(key, part):
    return decode_pair(key)[1].astype(jnp.bfloat16)


def draw_embeds(key, part):
    row_u = jax.random.uniform(jax.random.fold_in(key, 22), (TOKENS, 1), jnp.float32)
    col_u = jax.random.uniform(jax.random.fold_in(key, 23), (1, D), jnp.float32)
    trend = jnp.arange(D, dtype=jnp.float32)[None, :] / D
    base = jnp.clip(jax.random.normal(jax.random.fold_in(key, 21), (TOKENS, D), jnp.float32), -6.0, 6.0)
    col_scale = 10.0 ** (0.5 * trend + 0.5 * col_u)
    row_scale = 10.0 ** (row_u - 0.5)
    return (base * row_scale * col_scale).astype(jnp.bfloat16)


def draw_image_pos(key, part):

    def one_shard(shard):
        order = jax.random.permutation(jax.random.fold_in(key, 31 + shard), ROWS_DEV)
        picked = jnp.sort(order[:BATCH_DEV])
        return picked.astype(jnp.int32) + shard * ROWS_DEV
    shards = jnp.arange(IMGS // BATCH_DEV, dtype=jnp.int32)
    return jax.vmap(one_shard)(shards).reshape(IMGS).astype(jnp.int32)


def set_ends(array, key, least, largest):
    spot = [jax.random.randint(jax.random.fold_in(key, axis), (), 0, length) for axis, length in enumerate(array.shape)]
    widest = array.shape.index(max(array.shape))
    neighbour = spot[:widest] + [(spot[widest] + 1) % array.shape[widest]] + spot[widest + 1:]
    return array.at[tuple(spot)].set(least).at[tuple(neighbour)].set(largest)


def level_of(stream_key, dims, split, low, largest):
    loudness = 1.0
    for dim, blocks in split:
        draws = jax.random.uniform(jax.random.fold_in(jax.random.fold_in(stream_key, 6), dim), (blocks,), jnp.float32, low / len(split), largest / len(split))
        loudness = loudness * jnp.repeat(jnp.exp(draws), dims[dim] // blocks).reshape((-1,) + (1,) * (len(dims) - 1 - dim))
    return loudness


def assign_block(own_key, own, number, rows, number_of, top, bound, skew):
    sequence = jax.random.permutation(own_key, number_of)
    crowded, usual = load_shares(number_of, rows * top, bound, skew, True), load_shares(number_of, rows * top, bound, skew, False)
    places = jnp.arange(number_of)

    def named(tallies, rotation):
        used = int((tallies > 0).sum())
        fixed = max(1, used // 4)
        shifted = fixed + (places - fixed + rotation * (used - fixed)) % max(1, number_of - fixed)
        return jnp.zeros((number_of,), jnp.int32).at[sequence[jnp.where(places < fixed, places, shifted)]].set(jnp.asarray(tallies, jnp.int32))

    tallies = jnp.where(number % 4 == 0, named(crowded, number // 4), named(usual, number - number // 4 - 1))
    mixed = jax.random.permutation(jax.random.fold_in(own, 3), number_of)
    giver, sink = mixed[0:number_of // 2 * 2:2], mixed[1:number_of // 2 * 2:2]
    slack = jnp.minimum(tallies[giver] - 1, bound - tallies[sink]) // 2
    slack = jnp.where((giver == sequence[0]) | (sink == sequence[0]) | (tallies[sink] == 0), 0, jnp.maximum(slack, 0))
    shifted = jax.random.randint(jax.random.fold_in(own, 4), (number_of // 2,), 0, 1 << 20) % (slack + 1)
    tallies = tallies.at[giver].add(-shifted).at[sink].add(shifted)
    labels = jnp.searchsorted(jnp.cumsum(tallies), jnp.arange(rows * top), side="right").astype(jnp.int32)
    table = labels.reshape(top, rows).T
    table = table[jax.random.permutation(jax.random.fold_in(own, 1), rows)]
    rotation = jax.random.randint(jax.random.fold_in(own, 2), (rows, 1), 0, top)
    return jnp.take_along_axis(table, (jnp.arange(top)[None, :] + rotation) % top, axis=1)


def load_shares(count, total, bound, skew, full):
    loads = [(1 << 20) // math.isqrt(rank ** skew) + 1 for rank in range(1, count + 1)]
    largest = bound if full else min(bound, max(-(-total // count), total * loads[0] // sum(loads)))
    least = 1 if total - largest >= count - 1 else 0
    counts, rest = [largest] + [least] * (count - 1), total - largest - least * (count - 1)
    while rest > 0:
        candidates = [i for i in range(1, count) if counts[i] < largest] or [i for i in range(1, count) if counts[i] < bound]
        whole, remaining = sum([loads[i] for i in candidates]), rest
        for i in candidates:
            extra = min(bound - counts[i], max(1, remaining * loads[i] // whole), rest)
            counts[i] = counts[i] + extra
            rest = rest - extra
    return np.array(counts)


def scatter_about(rng, extent, scale, bound, pieces=(), kind=jnp.bfloat16):
    values = scale * jax.random.normal(rng, extent, jnp.float32)
    if pieces:
        values = values * level_of(rng, extent, pieces, -0.22, 0.18)
    return jnp.clip(values, -bound, bound).astype(kind)


def setup_inputs(seed: int = 0) -> dict:
    splits = jax.random.split(jax.random.key(seed), 14)
    embeds = draw_embeds(jax.random.fold_in(splits[13], 71), 0)
    image_feats = scatter_about(splits[1], (IMGS, C_VIS), 1.0, 6.0, ((0, 4),))
    image_pos = draw_image_pos(jax.random.fold_in(splits[13], 71), 0)
    proj_w = scatter_about(splits[3], (C_VIS, D), C_VIS ** -0.5, 0.0625, ((0, 4), (1, 4)))
    proj_b = scatter_about(splits[4], (D,), 0.5, 3.0, ((0, 4),))
    norm_gain = jnp.clip(1.0 + 0.18 * jax.random.normal(splits[5], (D,), jnp.float32), 0.099609375, 1.8984375).astype(jnp.bfloat16)
    kv_w = scatter_about(splits[6], (D, KVH * 2 * HEAD), D ** -0.5, 0.0625, ((0, 4),))
    prompt_lengths = jax.random.randint(splits[7], (PROMPTS,), PROMPT_LEN // 2, PROMPT_LEN + 1).astype(jnp.int32)
    page_owner_keys = jax.random.split(jax.random.fold_in(splits[8], 1), PAGES // PAGES_DEV)
    page_owner_turns = jax.random.permutation(jax.random.fold_in(splits[8], 3), PAGES // PAGES_DEV)
    page_owner = jax.vmap(lambda own, number: assign_block(jax.random.fold_in(splits[8], 2), own, number, PAGES_DEV, N_SEQ, 1, CAP, 2))(page_owner_keys, page_owner_turns).reshape((PAGES, 1))
    queries = draw_queries(jax.random.fold_in(splits[13], 71), 0)
    kv_cache = draw_kv_cache(jax.random.fold_in(splits[13], 71), 0)
    new_kv = scatter_about(splits[11], (IMGS, KVH * 2 * HEAD), 1.0, 5.0, ((0, 4), (1, 4)))
    cache_lengths = set_ends(jax.random.randint(splits[12], (IMGS,), 2, CACHE + 1), jax.random.fold_in(splits[12], 1), 2, CACHE).astype(jnp.int32)
    return dict(embeds=embeds, image_feats=image_feats, image_pos=image_pos, proj_w=proj_w, proj_b=proj_b, norm_gain=norm_gain, kv_w=kv_w, prompt_lengths=prompt_lengths, page_owner=page_owner, queries=queries, kv_cache=kv_cache, new_kv=new_kv, cache_lengths=cache_lengths)


def reference(embeds, image_feats, image_pos, proj_w, proj_b, norm_gain, kv_w, prompt_lengths, page_owner, queries, kv_cache, new_kv, cache_lengths):
    projected = jnp.dot(image_feats, proj_w, preferred_element_type=jnp.float32) + proj_b.astype(jnp.float32)
    image_hidden = jax.nn.gelu(projected, approximate=False).astype(jnp.bfloat16)
    hidden = embeds.at[image_pos].set(image_hidden)
    hidden_f32 = hidden.astype(jnp.float32)
    squares = lax.optimization_barrier(jnp.sum(hidden_f32 * hidden_f32, axis=1))
    row_scale = lax.rsqrt(squares / D + 1e-05)
    scaled = (hidden_f32 * norm_gain.astype(jnp.float32)).astype(jnp.bfloat16)
    kv_full = jnp.dot(scaled, kv_w, preferred_element_type=jnp.float32) * row_scale[:, None]
    positions = jnp.arange(TOKENS, dtype=jnp.int32)
    prompt_limit = prompt_lengths[positions // PROMPT_LEN]
    is_live = positions % PROMPT_LEN < prompt_limit
    kv_rows = jnp.where(is_live[:, None], kv_full, 0.0).astype(jnp.bfloat16)
    kv_pages = kv_rows.reshape(N_SEQ, PAGES_DEV, PAGE, KVH * 2 * HEAD)
    owners = page_owner[:, 0].reshape(N_SEQ, PAGES_DEV)
    one_hot = (owners[:, :, None] == jnp.arange(N_SEQ, dtype=jnp.int32)[None, None, :]).astype(jnp.int32)
    page_rank = lax.optimization_barrier(jnp.sum((jnp.cumsum(one_hot, axis=1) - one_hot) * one_hot, axis=2))
    slot_index = owners * CAP + page_rank
    selector = (slot_index[:, None, :] == jnp.arange(N_SEQ * CAP, dtype=jnp.int32)[None, :, None]).astype(jnp.float32)
    by_owner = jnp.einsum('sdp,spte->sdte', selector, kv_pages.astype(jnp.float32), precision=lax.Precision.HIGHEST).astype(jnp.bfloat16)
    sent_view = by_owner.reshape(N_SEQ * N_SEQ * CAP, PAGE, KVH * 2 * HEAD)
    received_view = by_owner.reshape(N_SEQ, N_SEQ, CAP, PAGE, KVH * 2 * HEAD).transpose(1, 0, 2, 3, 4).reshape(N_SEQ * N_SEQ * CAP, PAGE, KVH * 2 * HEAD)
    page_slots = jnp.concatenate([sent_view, received_view], axis=0)
    row_count = queries.shape[0]
    grouped = queries.astype(jnp.float32).reshape(row_count, KVH, QH // KVH, HEAD)
    cache_f32 = kv_cache.astype(jnp.float32).reshape(row_count, CACHE, KVH, 2 * HEAD)
    fresh_kv = new_kv.astype(jnp.float32).reshape(row_count, KVH, 2 * HEAD)
    scores = jnp.einsum('rgqh,rjgh->rgqj', grouped, cache_f32[..., :HEAD], precision=lax.Precision.HIGHEST) * HEAD ** (-0.5)
    in_cache = jnp.arange(CACHE, dtype=jnp.int32)[None, :] < cache_lengths[:, None]
    scores = jnp.where(in_cache[:, None, None, :], scores, -1e+30)
    own_score = jnp.einsum('rgqh,rgh->rgq', grouped, fresh_kv[..., :HEAD], precision=lax.Precision.HIGHEST) * HEAD ** (-0.5)
    row_max = jnp.maximum(lax.optimization_barrier(jnp.max(scores, axis=3)), own_score)
    weights = jnp.exp(scores - row_max[..., None])
    own_weight = jnp.exp(own_score - row_max)
    denominator = lax.optimization_barrier(jnp.sum(weights, axis=3)) + own_weight
    probability = lax.optimization_barrier((weights / denominator[..., None]).astype(jnp.bfloat16)).astype(jnp.float32)
    own_prob = lax.optimization_barrier((own_weight / denominator).astype(jnp.bfloat16)).astype(jnp.float32)
    attended = jnp.einsum('rgqj,rjgh->rgqh', probability, cache_f32[..., HEAD:], precision=lax.Precision.HIGHEST)
    attended = attended + own_prob[..., None] * fresh_kv[:, :, None, HEAD:]
    attended = attended.astype(jnp.bfloat16).reshape(row_count, QH * HEAD)
    row_states = jnp.concatenate([image_hidden, attended], axis=0)
    return (page_slots, row_states)
```

```python
import jax
import jax.numpy as jnp
from jax import lax
from jax.sharding import PartitionSpec as P

HEAD = 128
ROUTE_CHUNKS = 2


def gated(condition, action, empty_value, *operands):
    return lax.cond(condition, action, lambda *unused: empty_value, *operands)


def attend(queries, kv_cache, new_kv, cache_lengths):
    row_count = queries.shape[0]
    heads_kv = kv_cache.shape[2] // (2 * HEAD)
    grouped = queries.reshape(row_count, heads_kv, queries.shape[1] // (HEAD * heads_kv), HEAD)
    stored = kv_cache.reshape(row_count, kv_cache.shape[1], heads_kv, 2 * HEAD)
    fresh_kv = new_kv.reshape(row_count, heads_kv, 2 * HEAD)
    scores = jnp.einsum(
        "rgqh,rjgh->rgqj", grouped, stored[..., :HEAD], preferred_element_type=jnp.float32
    ) * HEAD ** (-0.5)
    in_cache = jnp.arange(stored.shape[1], dtype=jnp.int32)[None, :] < cache_lengths[:, None]
    scores = jnp.where(in_cache[:, None, None, :], scores, -1e30)
    own_score = jnp.einsum(
        "rgqh,rgh->rgq", grouped, fresh_kv[..., :HEAD], preferred_element_type=jnp.float32
    ) * HEAD ** (-0.5)
    row_max = jnp.maximum(jnp.max(scores, axis=3), own_score)
    weights = jnp.exp(scores - row_max[..., None])
    own_weight = jnp.exp(own_score - row_max)
    denominator = jnp.sum(weights, axis=3) + own_weight
    probability = (weights / denominator[..., None]).astype(jnp.bfloat16)
    own_prob = lax.optimization_barrier((own_weight / denominator).astype(jnp.bfloat16)).astype(
        jnp.float32
    )
    attended = jnp.einsum(
        "rgqj,rjgh->rgqh", probability, stored[..., HEAD:], preferred_element_type=jnp.float32
    )
    attended = attended + own_prob[..., None] * fresh_kv[:, :, None, HEAD:].astype(jnp.float32)
    return attended.astype(jnp.bfloat16).reshape(row_count, queries.shape[1])


def live_rows(positions, prompt_lengths, prompt_len):
    prompt_ids = positions // prompt_len
    match = prompt_ids[:, None] == jnp.arange(prompt_lengths.shape[0], dtype=jnp.int32)[None, :]
    limit = jnp.sum(jnp.where(match, prompt_lengths[None, :], 0), axis=1)
    return positions % prompt_len < limit


def per_device(
    embeds,
    image_feats,
    image_pos,
    proj_w,
    proj_b,
    norm_gain,
    kv_w,
    prompt_lengths,
    page_owner,
    queries,
    kv_cache,
    new_kv,
    cache_lengths,
):
    group_index = lax.axis_index("group")
    prefill = group_index == 0
    seq_index = lax.axis_index("seq")
    groups = lax.axis_size("group")
    seq_count = lax.axis_size("seq")
    mp_count = lax.axis_size("mp")
    token_rows, width_local = embeds.shape
    width = width_local * mp_count
    image_rows = image_feats.shape[0]
    prompt_len = token_rows * seq_count // prompt_lengths.shape[0]

    share_rows = image_rows // groups
    features = lax.dynamic_slice_in_dim(image_feats, group_index * share_rows, share_rows, axis=0)
    channels = proj_w.shape[0]
    shifts = [[(i, (i + k) % seq_count) for i in range(seq_count)] for k in range(seq_count)]
    pieces = [
        lax.dynamic_slice_in_dim(
            features, (seq_index + k) % seq_count * channels, channels, axis=1
        )
        for k in range(seq_count)
    ]
    pieces, norm_gain = lax.optimization_barrier((pieces, norm_gain))
    gathered = [pieces[0]]
    for k in range(1, seq_count):
        gathered.append(lax.ppermute(pieces[k], "seq", shifts[k]))
    spread = jnp.concatenate(gathered, axis=0)

    block_cols = kv_w.shape[1] // mp_count
    cols = block_cols // groups
    weight = jnp.concatenate(
        [
            lax.dynamic_slice_in_dim(kv_w, j * block_cols + group_index * cols, cols, axis=1)
            for j in range(mp_count)
        ],
        axis=1,
    )
    gain = norm_gain.astype(jnp.float32)
    text_f32 = embeds.astype(jnp.float32)
    text_scaled = (text_f32 * gain).astype(jnp.bfloat16)
    text_partial = jnp.dot(text_scaled, weight, preferred_element_type=jnp.float32)
    text_partial = text_partial.astype(jnp.bfloat16)
    text_kv = lax.psum_scatter(text_partial, "mp", scatter_dimension=1, tiled=True)
    text_squares = lax.psum(jnp.sum(text_f32 * text_f32, axis=1), "mp")

    spread, _ = lax.optimization_barrier((spread, text_partial))
    projected = jnp.dot(spread, proj_w, preferred_element_type=jnp.float32)
    projected = projected.reshape(seq_count, share_rows, width_local)
    bias, text_squares = lax.optimization_barrier((proj_b, text_squares))
    summed = projected[0] + bias.astype(jnp.float32)
    for k in range(1, seq_count):
        back = [(b, a) for a, b in shifts[k]]
        part = lax.ppermute(projected[k].astype(jnp.bfloat16), "seq", back)
        summed = summed + part.astype(jnp.float32)
    own_hidden = jax.nn.gelu(summed, approximate=False).astype(jnp.bfloat16)
    other_hidden = lax.ppermute(own_hidden, "group", [(0, 1), (1, 0)])
    image_hidden = jnp.concatenate(
        [
            jnp.where(prefill, own_hidden, other_hidden),
            jnp.where(prefill, other_hidden, own_hidden),
        ],
        axis=0,
    )

    image_f32 = image_hidden.astype(jnp.float32)
    image_scaled = (image_f32 * gain).astype(jnp.bfloat16)
    image_partial = jnp.dot(image_scaled, weight, preferred_element_type=jnp.float32)
    image_sum = jnp.sum(image_f32 * image_f32, axis=1)
    packed = jnp.concatenate(
        [
            jnp.concatenate([image_partial[:, j * cols : (j + 1) * cols] for j in range(mp_count)], axis=0),
            jnp.tile(jnp.broadcast_to(image_sum[:, None], (image_rows, HEAD)), (mp_count, 1)),
        ],
        axis=1,
    )
    packed, text_kv = lax.optimization_barrier((packed, text_kv))
    text_kv = text_kv.astype(jnp.float32)
    image_total = lax.psum_scatter(packed, "mp", scatter_dimension=0, tiled=True)
    image_scale = lax.rsqrt(image_total[:, cols] / width + 1e-05)
    image_live = live_rows(image_pos, prompt_lengths, prompt_len)
    image_kv = jnp.where(
        image_live[:, None], image_total[:, :cols] * image_scale[:, None], 0.0
    ).astype(jnp.bfloat16)

    positions = seq_index * token_rows + jnp.arange(token_rows, dtype=jnp.int32)
    is_live = live_rows(positions, prompt_lengths, prompt_len)
    placed = positions[:, None] == image_pos[None, :]
    is_image = jnp.any(placed, axis=1)
    text_scale = jnp.where(is_live, lax.rsqrt(text_squares / width + 1e-05), 0.0)
    image_part = jnp.dot(
        placed.astype(jnp.bfloat16), image_kv, preferred_element_type=jnp.float32
    )
    kv_rows = jnp.where(is_image[:, None], image_part, text_kv * text_scale[:, None]).astype(
        jnp.bfloat16
    )

    pages_dev = page_owner.shape[0]
    page = token_rows // pages_dev
    capacity = 2 * pages_dev // seq_count
    slots = seq_count * capacity
    owners = page_owner[:, 0]
    one_hot = (owners[:, None] == jnp.arange(seq_count, dtype=jnp.int32)[None, :]).astype(jnp.int32)
    page_rank = jnp.sum((jnp.cumsum(one_hot, axis=0) - one_hot) * one_hot, axis=1)
    slot_index = owners * capacity + page_rank
    selector = (jnp.arange(slots, dtype=jnp.int32)[:, None] == slot_index[None, :]).astype(
        jnp.bfloat16
    )
    step = cols // ROUTE_CHUNKS
    empty_rows = jnp.zeros(queries.shape, jnp.bfloat16)
    attended = gated(
        jnp.logical_not(prefill), attend, empty_rows, queries, kv_cache, new_kv, cache_lengths
    )
    own, other = [], []
    for chunk in range(ROUTE_CHUNKS):
        rows = kv_rows[:, chunk * step : (chunk + 1) * step].reshape(pages_dev, page * step)
        by_owner = jnp.dot(selector, rows, preferred_element_type=jnp.float32)
        by_owner = by_owner.astype(jnp.bfloat16).reshape(slots, page, step)
        arrived = lax.all_to_all(by_owner, "seq", split_axis=0, concat_axis=0, tiled=True)
        if chunk == ROUTE_CHUNKS - 1:
            arrived, attended = lax.optimization_barrier((arrived, attended))
        to_prefill = lax.ppermute(by_owner, "group", [(1, 0)])
        to_decode = lax.ppermute(arrived, "group", [(0, 1)])
        own.append(jnp.where(prefill, by_owner, arrived))
        other.append(jnp.where(prefill, to_prefill, to_decode))
    low = [jnp.where(prefill, a, b) for a, b in zip(own, other)]
    high = [jnp.where(prefill, b, a) for a, b in zip(own, other)]
    page_slots = jnp.concatenate(low + high, axis=2)

    row_states = jnp.where(prefill, image_hidden, attended)
    return (page_slots, row_states)


def solution(mesh):
    in_specs = (
        P("seq", "mp"),
        P("seq", None),
        P("seq"),
        P("seq", "mp"),
        P("mp"),
        P("mp"),
        P("mp", None),
        P(),
        P("seq", None),
        P("seq", "mp"),
        P("seq", None, "mp"),
        P("seq", "mp"),
        P("seq"),
    )
    out_specs = (P(("group", "seq"), None, "mp"), P(("group", "seq"), "mp"))
    return jax.shard_map(
        per_device, mesh=mesh, in_specs=in_specs, out_specs=out_specs, check_vma=False
    )
```

```python
import jax
import jax.numpy as jnp
from jax import lax
from jax.sharding import PartitionSpec as P

HEAD = 128
ROUTE_CHUNKS = 2


def gated(condition, action, empty_value, *operands):
    return lax.cond(condition, action, lambda *unused: empty_value, *operands)


def attend_head(queries, keys, values, fresh_key, fresh_value, in_cache):
    scores = jnp.einsum(
        "rqh,rjh->rqj", queries, keys, preferred_element_type=jnp.float32
    ) * HEAD ** (-0.5)
    scores = jnp.where(in_cache[:, None, :], scores, -1e30)
    own_score = jnp.einsum(
        "rqh,rh->rq", queries, fresh_key, preferred_element_type=jnp.float32
    ) * HEAD ** (-0.5)
    row_max = jnp.maximum(jnp.max(scores, axis=2), own_score)
    weights = jnp.exp(scores - row_max[..., None])
    own_weight = jnp.exp(own_score - row_max)
    denominator = jnp.sum(weights, axis=2) + own_weight
    probability = (weights / denominator[..., None]).astype(jnp.bfloat16)
    own_prob = lax.optimization_barrier((own_weight / denominator).astype(jnp.bfloat16)).astype(
        jnp.float32
    )
    attended = jnp.einsum("rqj,rjh->rqh", probability, values, preferred_element_type=jnp.float32)
    attended = attended + own_prob[..., None] * fresh_value[:, None, :].astype(jnp.float32)
    return attended.astype(jnp.bfloat16)


def attend(queries, kv_cache, new_kv, cache_lengths):
    row_count = queries.shape[0]
    heads_kv = kv_cache.shape[2] // (2 * HEAD)
    share = queries.shape[1] // heads_kv
    in_cache = jnp.arange(kv_cache.shape[1], dtype=jnp.int32)[None, :] < cache_lengths[:, None]
    heads = []
    for head in range(heads_kv):
        key, value, end = 2 * HEAD * head, 2 * HEAD * head + HEAD, 2 * HEAD * (head + 1)
        attended = attend_head(
            queries[:, head * share : (head + 1) * share].reshape(row_count, share // HEAD, HEAD),
            kv_cache[:, :, key:value],
            kv_cache[:, :, value:end],
            new_kv[:, key:value],
            new_kv[:, value:end],
            in_cache,
        )
        heads.append(attended.reshape(row_count, share))
    return jnp.concatenate(heads, axis=1)


def live_rows(positions, prompt_lengths, prompt_len):
    prompt_ids = positions // prompt_len
    match = prompt_ids[:, None] == jnp.arange(prompt_lengths.shape[0], dtype=jnp.int32)[None, :]
    limit = jnp.sum(jnp.where(match, prompt_lengths[None, :], 0), axis=1)
    return positions % prompt_len < limit


def per_device(
    embeds,
    image_feats,
    image_pos,
    proj_w,
    proj_b,
    norm_gain,
    kv_w,
    prompt_lengths,
    page_owner,
    queries,
    kv_cache,
    new_kv,
    cache_lengths,
):
    group_index = lax.axis_index("group")
    prefill = group_index == 0
    seq_index = lax.axis_index("seq")
    groups = lax.axis_size("group")
    seq_count = lax.axis_size("seq")
    mp_count = lax.axis_size("mp")
    token_rows, width_local = embeds.shape
    width = width_local * mp_count
    image_rows = image_feats.shape[0]
    prompt_len = token_rows * seq_count // prompt_lengths.shape[0]

    share_rows = image_rows // groups
    features = lax.dynamic_slice_in_dim(image_feats, group_index * share_rows, share_rows, axis=0)
    channels = proj_w.shape[0]
    shifts = [[(i, (i + k) % seq_count) for i in range(seq_count)] for k in range(seq_count)]
    pieces = [
        lax.dynamic_slice_in_dim(
            features, (seq_index + k) % seq_count * channels, channels, axis=1
        )
        for k in range(seq_count)
    ]
    pieces, norm_gain = lax.optimization_barrier((pieces, norm_gain))
    gathered = [pieces[0]]
    for k in range(1, seq_count):
        gathered.append(lax.ppermute(pieces[k], "seq", shifts[k]))
    spread = jnp.concatenate(gathered, axis=0)

    mp_index = lax.axis_index("mp")
    mp_shifts = [[(i, (i + k) % mp_count) for i in range(mp_count)] for k in range(mp_count)]
    block_cols = kv_w.shape[1] // mp_count
    cols = block_cols // groups
    weight = jnp.concatenate(
        [
            lax.dynamic_slice_in_dim(
                kv_w, (mp_index + k) % mp_count * block_cols + group_index * cols, cols, axis=1
            )
            for k in range(mp_count)
        ],
        axis=1,
    )
    gain = norm_gain.astype(jnp.float32)
    text_f32 = embeds.astype(jnp.float32)
    text_scaled = (text_f32 * gain).astype(jnp.bfloat16)
    text_partial = jnp.dot(text_scaled, weight, preferred_element_type=jnp.float32)
    text_partial = text_partial.astype(jnp.bfloat16)
    text_parts = [text_partial[:, :cols]]
    for k in range(1, mp_count):
        part = text_partial[:, k * cols : (k + 1) * cols]
        text_parts.append(lax.ppermute(part, "mp", mp_shifts[k]))
    text_squares = lax.psum(jnp.sum(text_f32 * text_f32, axis=1), "mp")

    spread, _ = lax.optimization_barrier((spread, text_partial))
    projected = jnp.dot(spread, proj_w, preferred_element_type=jnp.float32)
    projected = projected.reshape(seq_count, share_rows, width_local)
    bias, text_squares = lax.optimization_barrier((proj_b, text_squares))
    summed = projected[0] + bias.astype(jnp.float32)
    for k in range(1, seq_count):
        back = [(b, a) for a, b in shifts[k]]
        part = lax.ppermute(projected[k].astype(jnp.bfloat16), "seq", back)
        summed = summed + part.astype(jnp.float32)
    own_hidden = jax.nn.gelu(summed, approximate=False).astype(jnp.bfloat16)
    other_hidden = lax.ppermute(own_hidden, "group", [(0, 1), (1, 0)])
    image_hidden = jnp.concatenate(
        [
            jnp.where(prefill, own_hidden, other_hidden),
            jnp.where(prefill, other_hidden, own_hidden),
        ],
        axis=0,
    )

    image_f32 = image_hidden.astype(jnp.float32)
    image_scaled = (image_f32 * gain).astype(jnp.bfloat16)
    image_partial = jnp.dot(image_scaled, weight, preferred_element_type=jnp.float32)
    image_sum = jnp.sum(image_f32 * image_f32, axis=1)
    spare = jnp.broadcast_to(image_sum[:, None], (image_rows, HEAD))
    image_total = jnp.concatenate([image_partial[:, :cols], spare], axis=1)
    for k in range(1, mp_count):
        packed = jnp.concatenate([image_partial[:, k * cols : (k + 1) * cols], spare], axis=1)
        image_total = image_total + lax.ppermute(packed, "mp", mp_shifts[k])
    text_kv = text_parts[0].astype(jnp.float32)
    for part in text_parts[1:]:
        text_kv = text_kv + part.astype(jnp.float32)
    image_scale = lax.rsqrt(image_total[:, cols] / width + 1e-05)
    image_live = live_rows(image_pos, prompt_lengths, prompt_len)
    image_kv = jnp.where(
        image_live[:, None], image_total[:, :cols] * image_scale[:, None], 0.0
    ).astype(jnp.bfloat16)

    positions = seq_index * token_rows + jnp.arange(token_rows, dtype=jnp.int32)
    is_live = live_rows(positions, prompt_lengths, prompt_len)
    placed = positions[:, None] == image_pos[None, :]
    is_image = jnp.any(placed, axis=1)
    text_scale = jnp.where(is_live, lax.rsqrt(text_squares / width + 1e-05), 0.0)
    image_part = jnp.dot(
        placed.astype(jnp.bfloat16), image_kv, preferred_element_type=jnp.float32
    )
    kv_rows = jnp.where(is_image[:, None], image_part, text_kv * text_scale[:, None]).astype(
        jnp.bfloat16
    )

    pages_dev = page_owner.shape[0]
    page = token_rows // pages_dev
    capacity = 2 * pages_dev // seq_count
    slots = seq_count * capacity
    owners = page_owner[:, 0]
    one_hot = (owners[:, None] == jnp.arange(seq_count, dtype=jnp.int32)[None, :]).astype(jnp.int32)
    page_rank = jnp.sum((jnp.cumsum(one_hot, axis=0) - one_hot) * one_hot, axis=1)
    slot_index = owners * capacity + page_rank
    selector = (jnp.arange(slots, dtype=jnp.int32)[:, None] == slot_index[None, :]).astype(
        jnp.bfloat16
    )
    step = cols // ROUTE_CHUNKS
    empty_rows = jnp.zeros(queries.shape, jnp.bfloat16)
    attended = gated(
        jnp.logical_not(prefill), attend, empty_rows, queries, kv_cache, new_kv, cache_lengths
    )
    own, other = [], []
    for chunk in range(ROUTE_CHUNKS):
        rows = kv_rows[:, chunk * step : (chunk + 1) * step].reshape(pages_dev, page * step)
        if chunk == ROUTE_CHUNKS - 1:
            rows, attended = lax.optimization_barrier((rows, attended))
        by_owner = jnp.dot(selector, rows, preferred_element_type=jnp.float32)
        by_owner = by_owner.astype(jnp.bfloat16).reshape(slots, page, step)
        arrived = lax.all_to_all(by_owner, "seq", split_axis=0, concat_axis=0, tiled=True)
        to_prefill = lax.ppermute(by_owner, "group", [(1, 0)])
        to_decode = lax.ppermute(arrived, "group", [(0, 1)])
        own.append(jnp.where(prefill, by_owner, arrived))
        other.append(jnp.where(prefill, to_prefill, to_decode))
    low = [jnp.where(prefill, a, b) for a, b in zip(own, other)]
    high = [jnp.where(prefill, b, a) for a, b in zip(own, other)]
    page_slots = jnp.concatenate(low + high, axis=2)

    row_states = jnp.where(prefill, image_hidden, attended)
    return (page_slots, row_states)


def solution(mesh):
    in_specs = (
        P("seq", "mp"),
        P("seq", None),
        P("seq"),
        P("seq", "mp"),
        P("mp"),
        P("mp"),
        P("mp", None),
        P(),
        P("seq", None),
        P("seq", "mp"),
        P("seq", None, "mp"),
        P("seq", "mp"),
        P("seq"),
    )
    out_specs = (P(("group", "seq"), None, "mp"), P(("group", "seq"), "mp"))
    return jax.shard_map(
        per_device, mesh=mesh, in_specs=in_specs, out_specs=out_specs, check_vma=False
    )
```
